32 devices in a mesh: gx: 4 (over z), gy: 8 (over y, x, core).
Axes of the slice: x: 2, y: 2, z: 4, core: 2. Of those that a mesh axis runs over, the one named last changes fastest.
Arguments:
- velocity: float32 [3, 32, 64, 1024], P(None, None, 'gx', 'gy'), may hold values from -6 to 6
- old_tendency: float32 [3, 32, 64, 1024], P(None, None, 'gx', 'gy'), may hold values from -6 to 6
- obstacle: int32 [32, 64, 1024], P(None, 'gx', 'gy'), may hold values 0 or 1
Outputs:
- corrected: float32 [3, 32, 64, 1024], P(None, None, 'gx', 'gy')
- pressure: float32 [32, 64, 1024], P(None, 'gx', 'gy')
The draws below stay inside these ranges and needn't reach their ends.
Inputs may be any that keep to these rules, and one draw needn't show every extreme that they name: `obstacle`: 1 marks a building cell, 0 a fluid cell.
All inputs are finite; a program needn't handle non-finite values. No bound on the sum of `obstacle` on one device may be relied on, other than what follows from the above.
Results may differ from the reference program's by a relative error of at most 0.00002.
Values sent between devices are 32-bit elements; how exact they have to be, the bound alone decides.
A program may use at most 128 MiB of HBM per device.

```python
import jax
import jax.numpy as jnp

NZ = 32
LEVELS = 3
SWEEPS = 2
COARSE_SWEEPS = 8
NX = 64
NY = 1024


def with_ends(entries, stream_key, least, largest):
    dims = entries.shape
    spot = [jax.random.randint(jax.random.fold_in(stream_key, axis), (), 0, dims[axis]) for axis in range(len(dims))]
    entries = entries.at[tuple(spot)].set(least)
    longest = dims.index(max(dims))
    spot[longest] = (spot[longest] + 1) % dims[longest]
    return entries.at[tuple(spot)].set(largest)


def level_of(own_key, shape, cuts, low, top_value):
    def one(dim, parts):
        heights = jax.random.uniform(jax.random.fold_in(jax.random.fold_in(own_key, 6), dim), (parts,), jnp.float32, low / len(cuts), top_value / len(cuts))
        return jnp.repeat(jnp.exp(heights), shape[dim] // parts).reshape((-1,) + (1,) * (len(shape) - dim - 1))

    gain = one(*cuts[0])
    for cut in cuts[1:]:
        gain = gain * one(*cut)
    return gain


def noise(rng, dims, spread, bound, cuts=(), held_as=jnp.bfloat16):
    values = jax.random.normal(rng, dims, jnp.float32) * spread
    if len(cuts) > 0:
        values = level_of(rng, dims, cuts, -0.22, 0.18) * values
    return jnp.clip(values, min=-bound, max=bound).astype(held_as)


def setup_inputs(seed: int = 0) -> dict:
    key_list = jax.random.split(jax.random.key(seed), 4)
    velocity = noise(key_list[0], (3, NZ, NX, NY), 1.0, 6.0, ((2, 4), (3, 8)), jnp.float32)
    old_tendency = noise(key_list[1], (3, NZ, NX, NY), 1.0, 6.0, ((2, 4), (3, 8)), jnp.float32)
    obstacle = with_ends((jax.random.randint(key_list[2], (NZ, NX, NY), 0, 6) < 1).astype(jnp.int32), jax.random.fold_in(key_list[2], 1), 0, 1)
    return {"velocity": velocity, "old_tendency": old_tendency, "obstacle": obstacle}


VISCOSITY = 0.1
TIME_STEP = 0.25
WEIGHT_NEW = 15.0 / 16.0
WEIGHT_OLD = -25.0 / 48.0
HELMHOLTZ = 1.0e-4


def vertical_pair(field):
    zeros_layer = jnp.zeros_like(field[..., :1, :, :])
    upper_cell = jnp.concatenate([field[..., 1:, :, :], zeros_layer], axis=-3)
    lower_cell = jnp.concatenate([zeros_layer, field[..., :-1, :, :]], axis=-3)
    return upper_cell, lower_cell


def vertical_count(size_z):
    layers = jnp.arange(size_z)
    above_ok = (layers < size_z - 1).astype(jnp.float32)
    below_ok = (layers > 0).astype(jnp.float32)
    return (above_ok + below_ok)[:, None, None]


def parity(size_z, size_x, size_y, start_x, start_y):
    layer_z = jnp.arange(size_z, dtype=jnp.int32)[:, None, None]
    row_x = (jnp.arange(size_x, dtype=jnp.int32) + start_x)[None, :, None]
    col_y = (jnp.arange(size_y, dtype=jnp.int32) + start_y)[None, None, :]
    return (layer_z + row_x + col_y) % 2


def gather_neighbours(extended):
    center = extended[:, 1:-1, 1:-1]
    upper_cell, lower_cell = vertical_pair(center)
    neighbours = extended[:, 2:, 1:-1] + extended[:, :-2, 1:-1] + extended[:, 1:-1, 2:] + extended[:, 1:-1, :-2] + upper_cell + lower_cell
    return center, neighbours


def relax_update(extended, source, spacing):
    center, neighbours = gather_neighbours(extended)
    diagonal = HELMHOLTZ + (4.0 + vertical_count(center.shape[0])) / spacing
    return (source + neighbours / spacing) / diagonal


def apply_operator(extended, spacing):
    center, neighbours = gather_neighbours(extended)
    diagonal = HELMHOLTZ + (4.0 + vertical_count(center.shape[0])) / spacing
    return diagonal * center - neighbours / spacing


def wrapped(field):
    return jnp.pad(field, ((0, 0), (1, 1), (1, 1)), mode="wrap")


def restrict(field):
    size_z, size_x, size_y = field.shape
    return field.reshape(size_z // 2, 2, size_x // 2, 2, size_y // 2, 2).mean(axis=(1, 3, 5))


def prolong(field):
    return jnp.repeat(jnp.repeat(jnp.repeat(field, 2, axis=0), 2, axis=1), 2, axis=2)


def global_sweep(field, source, spacing, colour):
    for shade in (0, 1):
        field = jnp.where(colour == shade, relax_update(wrapped(field), source, spacing), field)
    return field


def global_cycle(source, level):
    spacing = float(4 ** level)
    size_z, size_x, size_y = source.shape
    colour = parity(size_z, size_x, size_y, 0, 0)
    field = jnp.zeros_like(source)
    if level == LEVELS:
        for repeat_idx in range(COARSE_SWEEPS):
            field = global_sweep(field, source, spacing, colour)
        return field
    for repeat_idx in range(SWEEPS):
        field = global_sweep(field, source, spacing, colour)
    remain = source - apply_operator(wrapped(field), spacing)
    field = field + prolong(global_cycle(restrict(remain), level + 1))
    for repeat_idx in range(SWEEPS):
        field = global_sweep(field, source, spacing, colour)
    return field


def momentum(velocity, plus_x, minus_x, plus_y, minus_y, old_tendency, fluid):
    upper_cell, lower_cell = vertical_pair(velocity)
    advect = velocity[0] * (plus_x - minus_x) * 0.5 + velocity[1] * (plus_y - minus_y) * 0.5 + velocity[2] * (upper_cell - lower_cell) * 0.5
    diffuse = plus_x + minus_x + plus_y + minus_y + upper_cell + lower_cell - 6.0 * velocity
    tendency = VISCOSITY * diffuse - advect
    return fluid * (velocity + TIME_STEP * (WEIGHT_NEW * tendency + WEIGHT_OLD * old_tendency))


def divergence_of(east_u, west_u, north_v, south_v, predicted):
    upper_cell, lower_cell = vertical_pair(predicted[2])
    return 0.5 * ((east_u - west_u) + (north_v - south_v) + (upper_cell - lower_cell))


def correct(predicted, pressure_ext, pressure, fluid):
    upper_cell, lower_cell = vertical_pair(pressure)
    gradient = jnp.stack([
        0.5 * (pressure_ext[:, 2:, 1:-1] - pressure_ext[:, :-2, 1:-1]),
        0.5 * (pressure_ext[:, 1:-1, 2:] - pressure_ext[:, 1:-1, :-2]),
        0.5 * (upper_cell - lower_cell)])
    return fluid * (predicted - TIME_STEP * gradient)


def reference(velocity, old_tendency, obstacle):
    fluid = (1 - obstacle).astype(jnp.float32)
    predicted = momentum(velocity, jnp.roll(velocity, -1, axis=2), jnp.roll(velocity, 1, axis=2),
                         jnp.roll(velocity, -1, axis=3), jnp.roll(velocity, 1, axis=3), old_tendency, fluid)
    divergence = divergence_of(jnp.roll(predicted[0], -1, axis=1), jnp.roll(predicted[0], 1, axis=1),
                               jnp.roll(predicted[1], -1, axis=2), jnp.roll(predicted[1], 1, axis=2), predicted)
    source = -divergence / TIME_STEP
    pressure = global_cycle(source, 0)
    corrected = correct(predicted, wrapped(pressure), pressure, fluid)
    return corrected, pressure
```

```python
import functools

import jax
import jax.numpy as jnp
from jax import lax
from jax.experimental import pallas as pl
from jax.experimental.pallas import tpu as pltpu
from jax.sharding import PartitionSpec as P

LEVELS = 3
SWEEPS = 2
COARSE_SWEEPS = 8
VISCOSITY = 0.1
TIME_STEP = 0.25
WEIGHT_NEW = 15.0 / 16.0
WEIGHT_OLD = -25.0 / 48.0
HELMHOLTZ = 0.0001

LANES = 128
SUB = 8
HALO_X = 8
HALO_Y = 24
MESH = pl.DeviceIdType.MESH


def iota2(shape, dim):
    return lax.broadcasted_iota(jnp.int32, shape, dim)


def restrict_matrix(rows, cols, nz, period):
    i, o = iota2((rows, cols), 0), iota2((rows, cols), 1)
    o = o % period
    half = nz // 2
    hit = ((i // nz) // 2 == o // half) & ((i % nz) // 2 == o % half)
    return jnp.where(hit, 0.125, 0.0).astype(jnp.float32)


def prolong_matrix(rows, cols, nz):
    i, o = iota2((rows, cols), 0), iota2((rows, cols), 1)
    half = nz // 2
    hit = ((o // nz) // 2 == i // half) & ((o % nz) // 2 == i % half)
    return jnp.where(hit, 1.0, 0.0).astype(jnp.float32)


def mm(a, b):
    return jnp.dot(a, b, precision=lax.Precision.HIGHEST, preferred_element_type=jnp.float32)


class Level:
    def __init__(self, level, nz):
        self.nz = nz
        self.scale = 1.0 / float(4**level)
        lane = iota2((SUB, LANES), 1)
        row = iota2((SUB, LANES), 0)
        self.lane = lane
        self.row = row
        z = lane % nz
        self.not_top = z < nz - 1
        self.not_bottom = z > 0
        parity = (z + lane // nz + row) % 2
        self.colour = [parity == 0, parity == 1]
        edge = (z == 0) | (z == nz - 1)
        diag_in = HELMHOLTZ + 6.0 * self.scale
        diag_edge = HELMHOLTZ + 5.0 * self.scale
        self.diag = jnp.where(edge, diag_edge, diag_in).astype(jnp.float32)
        self.inv = jnp.where(edge, 1.0 / diag_edge, 1.0 / diag_in).astype(jnp.float32)
        self.take = jnp.where(
            edge, self.scale / diag_edge, self.scale / diag_in
        ).astype(jnp.float32)

    def x_plus(self, tiles, t):
        n = len(tiles)
        both = tiles[t] if n == 1 else jnp.where(self.lane < self.nz, tiles[(t + 1) % n], tiles[t])
        return pltpu.roll(both, LANES - self.nz, 1)

    def x_minus(self, tiles, t):
        n = len(tiles)
        last = self.lane >= LANES - self.nz
        both = tiles[t] if n == 1 else jnp.where(last, tiles[(t - 1) % n], tiles[t])
        return pltpu.roll(both, self.nz, 1)

    def y_plus(self, tile, following):
        return pltpu.roll(jnp.where(self.row == 0, following, tile), SUB - 1, 0)

    def y_minus(self, tile, previous):
        return pltpu.roll(jnp.where(self.row == SUB - 1, previous, tile), 1, 0)

    def z_plus(self, tile):
        return jnp.where(self.not_top, pltpu.roll(tile, LANES - 1, 1), 0.0)

    def z_minus(self, tile):
        return jnp.where(self.not_bottom, pltpu.roll(tile, 1, 1), 0.0)


def tile_of(t):
    return slice(t * LANES, (t + 1) * LANES)


def row_loop(tiles, unroll, body):
    while tiles % unroll:
        unroll -= 1

    def step(i, carry):
        for k in range(unroll):
            body(pl.multiple_of((i * unroll + k) * SUB, SUB))
        return carry

    lax.fori_loop(0, tiles // unroll, step, 0)


def neighbours(lv, p, r, tiles, t):
    cols = tile_of(t)
    here = tiles[t]
    up = lv.y_plus(here, p[pl.ds(r + 2 * SUB, SUB), cols])
    down = lv.y_minus(here, p[pl.ds(r, SUB), cols])
    return (
        lv.x_plus(tiles, t)
        + lv.x_minus(tiles, t)
        + up
        + down
        + lv.z_plus(here)
        + lv.z_minus(here)
    )


def wrap_rows(p):
    rows = p.shape[0]
    p[0:SUB, :] = p[rows - 2 * SUB : rows - SUB, :]
    p[rows - SUB : rows, :] = p[SUB : 2 * SUB, :]


def first_half(lv, p, f, unroll):
    def body(r):
        for t in range(p.shape[1] // LANES):
            p[pl.ds(r + SUB, SUB), tile_of(t)] = jnp.where(
                lv.colour[0], f[pl.ds(r, SUB), tile_of(t)] * lv.inv, 0.0
            )

    row_loop(f.shape[0] // SUB, unroll, body)


def half_sweep(lv, p, f, colour, unroll, wrap):
    if wrap:
        wrap_rows(p)
    count = p.shape[1] // LANES

    def body(r):
        tiles = [p[pl.ds(r + SUB, SUB), tile_of(t)] for t in range(count)]
        for t in range(count):
            total = neighbours(lv, p, r, tiles, t)
            new = f[pl.ds(r, SUB), tile_of(t)] * lv.inv + total * lv.take
            p[pl.ds(r + SUB, SUB), tile_of(t)] = jnp.where(lv.colour[colour], new, tiles[t])

    row_loop(f.shape[0] // SUB, unroll, body)


def presmooth(lv, p, f, sweeps, unroll, wrap):
    first_half(lv, p, f, unroll)
    for k in range(1, 2 * sweeps):
        half_sweep(lv, p, f, k % 2, unroll, wrap)


def postsmooth(lv, p, f, unroll, wrap):
    for k in range(2 * SWEEPS):
        half_sweep(lv, p, f, k % 2, unroll, wrap)


def residual(lv, p, f, out, first, last, unroll, wrap):
    if wrap:
        wrap_rows(p)
    count = p.shape[1] // LANES

    def body(r):
        tiles = [p[pl.ds(r + SUB, SUB), tile_of(t)] for t in range(count)]
        for t in range(first, last):
            total = neighbours(lv, p, r, tiles, t)
            out[pl.ds(r, SUB), tile_of(t - first)] = f[pl.ds(r, SUB), tile_of(t)] - (
                lv.diag * tiles[t] - lv.scale * total
            )

    row_loop(f.shape[0] // SUB, unroll, body)


def restrict_rows(value, pairs, start, count, emit):
    for t in range(value.shape[1] // LANES):
        pairs[t, 0 : value.shape[0], :] = value[:, tile_of(t)]
        emit(
            t,
            pairs[t, pl.ds(start, count, stride=2), :]
            + pairs[t, pl.ds(start + 1, count, stride=2), :],
        )


def prolong_rows(value, pairs, p, first):
    rows = value.shape[0]
    for k in range(value.shape[1] // LANES):
        t = first + k
        pairs[t, pl.ds(0, rows, stride=2), :] = value[:, tile_of(k)]
        pairs[t, pl.ds(1, rows, stride=2), :] = value[:, tile_of(k)]
        p[SUB : SUB + 2 * rows, tile_of(t)] += pairs[t, 0 : 2 * rows, :]


def kernel(
    nx_dev, ny_dev, nz, nx, ny,
    vel_in, old_in, obs_in, cor_out, pre_out,
    vel, old, fluid, edge, edge_in, pred,
    f0, p0, r0, f1, p1, r1, f2, p2, r2, f3, p3, pairs,
    send_sem, recv_sem,
):
    gx, gy = lax.axis_index("gx"), lax.axis_index("gy")

    def device(dx, dy):
        return (lax.rem(gx + dx + nx_dev, nx_dev), lax.rem(gy + dy + ny_dev, ny_dev))

    peers = [(d, 0) for d in range(1, nx_dev)] + [(0, d) for d in range(1, ny_dev)]
    peers += [(a, b) for a in (-1, 1) for b in (-1, 1)]
    barrier = pltpu.get_barrier_semaphore()
    for dx, dy in peers:
        pl.semaphore_signal(barrier, inc=1, device_id=device(dx, dy), device_id_type=MESH)

    number = [0]

    def send(src, dst, dx, dy):
        k = number[0]
        number[0] += 1
        copy = pltpu.make_async_remote_copy(
            src_ref=src, dst_ref=dst, send_sem=send_sem.at[k], recv_sem=recv_sem.at[k],
            device_id=device(dx, dy), device_id_type=MESH,
        )
        copy.start()
        return copy

    per = LANES // nz
    blocks = nx // per
    width = blocks * LANES
    lv0 = Level(0, nz)
    lane = lv0.lane

    def load_tile(ref, base, t):
        rows = [ref[pl.ds(base + t * per + i, nz, stride=nx), :] for i in range(per)]
        return jnp.concatenate(rows, axis=0).T

    for c in range(3):
        for t in range(blocks):
            vel[c, SUB : SUB + ny, tile_of(t + 1)] = load_tile(vel_in, c * nz * nx, t)

    pltpu_wait = functools.partial(pl.semaphore_wait, barrier)
    pltpu_wait(len(peers))

    def join(high):
        parts = []
        for c in range(3):
            source = vel[c, SUB : SUB + ny, tile_of(blocks if high else 1)]
            start = LANES - nz if high else 0
            parts.append(pltpu.roll(source, (c * nz - start) % LANES, 1))
        wide = iota2((ny, LANES), 1)
        return jnp.where(wide < nz, parts[0], jnp.where(wide < 2 * nz, parts[1], parts[2]))

    copies = [
        send(vel.at[:, ny : ny + SUB, LANES : LANES + width], vel.at[:, 0:SUB, LANES : LANES + width], 0, 1),
        send(
            vel.at[:, SUB : 2 * SUB, LANES : LANES + width],
            vel.at[:, SUB + ny : 2 * SUB + ny, LANES : LANES + width], 0, -1,
        ),
    ]
    edge[0] = join(True)
    copies.append(send(edge.at[0], edge_in.at[0], 1, 0))
    edge[1] = join(False)
    copies.append(send(edge.at[1], edge_in.at[1], -1, 0))

    for c in range(3):
        for t in range(blocks):
            old[c, :, tile_of(t)] = load_tile(old_in, c * nz * nx, t)
    for t in range(blocks):
        fluid[:, tile_of(t)] = (1 - load_tile(obs_in, 0, t)).astype(jnp.float32)
    for copy in copies:
        copy.wait()
    for c in range(3):
        vel[c, SUB : SUB + ny, tile_of(0)] = pltpu.roll(edge_in[0], (LANES - nz - c * nz) % LANES, 1)
        vel[c, SUB : SUB + ny, tile_of(blocks + 1)] = pltpu.roll(edge_in[1], (-c * nz) % LANES, 1)

    def momentum(r):
        here = [
            [vel[c, pl.ds(r + SUB, SUB), tile_of(t)] for t in range(blocks + 2)] for c in range(3)
        ]
        for t in range(1, blocks + 1):
            cols = tile_of(t)
            wet = fluid[pl.ds(r, SUB), tile_of(t - 1)]
            for c in range(3):
                q = here[c][t]
                xp, xm = lv0.x_plus(here[c], t), lv0.x_minus(here[c], t)
                yp = lv0.y_plus(q, vel[c, pl.ds(r + 2 * SUB, SUB), cols])
                ym = lv0.y_minus(q, vel[c, pl.ds(r, SUB), cols])
                zp, zm = lv0.z_plus(q), lv0.z_minus(q)
                advect = 0.5 * (
                    here[0][t] * (xp - xm) + here[1][t] * (yp - ym) + here[2][t] * (zp - zm)
                )
                diffuse = xp + xm + yp + ym + zp + zm - 6.0 * q
                tendency = VISCOSITY * diffuse - advect
                pred[c, pl.ds(r + SUB, SUB), cols] = wet * (
                    q
                    + TIME_STEP
                    * (WEIGHT_NEW * tendency + WEIGHT_OLD * old[c, pl.ds(r, SUB), tile_of(t - 1)])
                )

    row_loop(ny // SUB, 1, momentum)

    inner = slice(LANES, LANES + width)
    copies = [
        send(pred.at[0, SUB : SUB + ny, tile_of(blocks)], pred.at[0, SUB : SUB + ny, tile_of(0)], 1, 0),
        send(pred.at[0, SUB : SUB + ny, tile_of(1)], pred.at[0, SUB : SUB + ny, tile_of(blocks + 1)], -1, 0),
        send(pred.at[1, ny : ny + SUB, inner], pred.at[1, 0:SUB, inner], 0, 1),
        send(pred.at[1, SUB : 2 * SUB, inner], pred.at[1, SUB + ny : 2 * SUB + ny, inner], 0, -1),
    ]
    for copy in copies:
        copy.wait()

    side = HALO_X // per
    hx = side * LANES

    def divergence(r):
        u = [pred[0, pl.ds(r + SUB, SUB), tile_of(t)] for t in range(blocks + 2)]
        for t in range(1, blocks + 1):
            cols = tile_of(t)
            v = pred[1, pl.ds(r + SUB, SUB), cols]
            w = pred[2, pl.ds(r + SUB, SUB), cols]
            v_plus = lv0.y_plus(v, pred[1, pl.ds(r + 2 * SUB, SUB), cols])
            v_minus = lv0.y_minus(v, pred[1, pl.ds(r, SUB), cols])
            total = (
                (lv0.x_plus(u, t) - lv0.x_minus(u, t))
                + (v_plus - v_minus)
                + (lv0.z_plus(w) - lv0.z_minus(w))
            )
            f0[pl.ds(r + HALO_Y, SUB), tile_of(t - 1 + side)] = total * (-0.5 / TIME_STEP)

    row_loop(ny // SUB, 1, divergence)

    span = {
        0: (slice(HALO_Y, HALO_Y + ny), slice(HALO_Y, HALO_Y + ny)),
        1: (slice(ny, ny + HALO_Y), slice(0, HALO_Y)),
        -1: (slice(HALO_Y, 2 * HALO_Y), slice(HALO_Y + ny, 2 * HALO_Y + ny)),
    }
    cross = {
        0: (slice(hx, hx + width), slice(hx, hx + width)),
        1: (slice(width, width + hx), slice(0, hx)),
        -1: (slice(hx, 2 * hx), slice(hx + width, 2 * hx + width)),
    }
    copies = []
    for dx, dy in ((1, 0), (-1, 0), (0, 1), (0, -1), (1, 1), (1, -1), (-1, 1), (-1, -1)):
        copies.append(
            send(f0.at[span[dy][0], cross[dx][0]], f0.at[span[dy][1], cross[dx][1]], dx, dy)
        )
    lv1, lv2, lv3 = Level(1, nz // 2), Level(2, nz // 4), Level(3, nz // 8)
    zero_rows = jnp.zeros((SUB, p0.shape[1]), jnp.float32)
    p0[0:SUB, :] = zero_rows
    p0[p0.shape[0] - SUB :, :] = zero_rows
    p1[0:SUB, :] = zero_rows[:, : p1.shape[1]]
    p1[p1.shape[0] - SUB :, :] = zero_rows[:, : p1.shape[1]]
    for copy in copies:
        copy.wait()

    presmooth(lv0, p0, f0, SWEEPS, 1, False)
    residual(lv0, p0, f0, r0, side, side + blocks, 1, False)
    rows1 = f1.shape[0]
    down1 = mm(r0[...], restrict_matrix(width, LANES, nz, LANES))

    def emit1(t, value):
        f1[:, tile_of(t)] = value

    restrict_rows(down1, pairs, 0, rows1, emit1)

    copies = [
        send(f1.at[:, tile_of(0)], f1.at[:, tile_of(j)], nx_dev - j, 0) for j in range(1, nx_dev)
    ]
    for copy in copies:
        copy.wait()
    presmooth(lv1, p1, f1, SWEEPS, 1, False)
    residual(lv1, p1, f1, r1, 0, nx_dev, 1, False)
    cols2 = f2.shape[1]
    down2 = mm(r1[...], restrict_matrix(r1.shape[1], cols2, nz // 2, cols2))
    own2 = ny // 4

    def emit2(t, value):
        f2[0:own2, tile_of(t)] = value

    restrict_rows(down2, pairs, HALO_Y // 2, own2, emit2)
    copies = [
        send(f2.at[0:own2, :], f2.at[j * own2 : (j + 1) * own2, :], 0, ny_dev - j)
        for j in range(1, ny_dev)
    ]
    for copy in copies:
        copy.wait()

    presmooth(lv2, p2, f2, SWEEPS, 8, True)
    residual(lv2, p2, f2, r2, 0, cols2 // LANES, 8, True)
    down3 = mm(r2[...], restrict_matrix(cols2, f3.shape[1], nz // 4, cols2 // 4))

    def emit3(t, value):
        f3[:, tile_of(t)] = value

    restrict_rows(down3, pairs, 0, f3.shape[0], emit3)
    presmooth(lv3, p3, f3, COARSE_SWEEPS, 16, True)
    rows3 = f3.shape[0]
    prolong_rows(
        mm(p3[SUB : SUB + rows3, :], prolong_matrix(p3.shape[1], cols2, nz // 4)), pairs, p2, 0
    )
    postsmooth(lv2, p2, f2, 8, True)
    wrap_rows(p2)

    first2 = SUB - HALO_Y // 4
    window = p2[first2 : first2 + rows1 // 2, :]
    prolong_rows(mm(window, prolong_matrix(cols2, r1.shape[1], nz // 2)), pairs, p1, 0)
    postsmooth(lv1, p1, f1, 1, False)

    lift = prolong_matrix(LANES, width, nz)
    body_rows = slice(SUB, SUB + rows1)
    prolong_rows(mm(p1[body_rows, tile_of(nx_dev - 1)], lift[:, width - hx :]), pairs, p0, 0)
    prolong_rows(mm(p1[body_rows, tile_of(0)], lift), pairs, p0, side)
    prolong_rows(mm(p1[body_rows, tile_of(1)], lift[:, :hx]), pairs, p0, side + blocks)
    postsmooth(lv0, p0, f0, 1, False)

    low = SUB + HALO_Y

    def correct(r):
        here = [
            p0[pl.ds(r + low, SUB), tile_of(t)] for t in range(side - 1, side + blocks + 1)
        ]
        for t in range(1, blocks + 1):
            cols = tile_of(t + side - 1)
            slope = (
                lv0.x_plus(here, t) - lv0.x_minus(here, t),
                lv0.y_plus(here[t], p0[pl.ds(r + low + SUB, SUB), cols])
                - lv0.y_minus(here[t], p0[pl.ds(r + low - SUB, SUB), cols]),
                lv0.z_plus(here[t]) - lv0.z_minus(here[t]),
            )
            wet = fluid[pl.ds(r, SUB), tile_of(t - 1)]
            for c in range(3):
                old[c, pl.ds(r, SUB), tile_of(t - 1)] = wet * (
                    pred[c, pl.ds(r + SUB, SUB), tile_of(t)] - (0.5 * TIME_STEP) * slope[c]
                )

    row_loop(ny // SUB, 1, correct)

    def store_tile(ref, base, t, value):
        turned = value.T
        for i in range(per):
            ref[pl.ds(base + t * per + i, nz, stride=nx), :] = turned[i * nz : (i + 1) * nz, :]

    for t in range(blocks):
        store_tile(pre_out, 0, t, p0[low : low + ny, tile_of(t + side)])
    for c in range(3):
        for t in range(blocks):
            store_tile(cor_out, c * nz * nx, t, old[c, :, tile_of(t)])


def body(nx_dev, ny_dev, velocity, old_tendency, obstacle):
    _, nz, nx, ny = velocity.shape
    rows0 = ny + 2 * HALO_Y
    wide0 = (nx + 2 * HALO_X) * nz
    width = nx * nz
    rows1, wide1 = rows0 // 2, nx_dev * (nx // 2) * (nz // 2)
    rows2, wide2 = ny_dev * ny // 4, nx_dev * (nx // 4) * (nz // 4)
    rows3 = rows2 // 2
    wide3 = max(LANES, wide2 // 4)
    tall = max(rows0, rows1, rows2)
    count = max(wide0, wide1, wide2, wide3) // LANES
    copies = 4 + 4 + 8 + (nx_dev - 1) + (ny_dev - 1)
    f32 = jnp.float32
    out = pl.pallas_call(
        functools.partial(kernel, nx_dev, ny_dev, nz, nx, ny),
        out_shape=(
            jax.ShapeDtypeStruct((3 * nz * nx, ny), f32),
            jax.ShapeDtypeStruct((nz * nx, ny), f32),
        ),
        in_specs=[pl.BlockSpec(memory_space=pltpu.VMEM)] * 3,
        out_specs=[pl.BlockSpec(memory_space=pltpu.VMEM)] * 2,
        scratch_shapes=[
            pltpu.VMEM((3, ny + 2 * SUB, width + 2 * LANES), f32),
            pltpu.VMEM((3, ny, width), f32),
            pltpu.VMEM((ny, width), f32),
            pltpu.VMEM((2, ny, LANES), f32),
            pltpu.VMEM((2, ny, LANES), f32),
            pltpu.VMEM((3, ny + 2 * SUB, width + 2 * LANES), f32),
            pltpu.VMEM((rows0, wide0), f32),
            pltpu.VMEM((rows0 + 2 * SUB, wide0), f32),
            pltpu.VMEM((rows0, width), f32),
            pltpu.VMEM((rows1, wide1), f32),
            pltpu.VMEM((rows1 + 2 * SUB, wide1), f32),
            pltpu.VMEM((rows1, wide1), f32),
            pltpu.VMEM((rows2, wide2), f32),
            pltpu.VMEM((rows2 + 2 * SUB, wide2), f32),
            pltpu.VMEM((rows2, wide2), f32),
            pltpu.VMEM((rows3, wide3), f32),
            pltpu.VMEM((rows3 + 2 * SUB, wide3), f32),
            pltpu.VMEM((count, tall, LANES), f32),
            pltpu.SemaphoreType.DMA((copies,)),
            pltpu.SemaphoreType.DMA((copies,)),
        ],
        compiler_params=pltpu.CompilerParams(
            collective_id=0, has_side_effects=True, vmem_limit_bytes=60 * 1024 * 1024
        ),
    )(
        velocity.reshape(3 * nz * nx, ny),
        old_tendency.reshape(3 * nz * nx, ny),
        obstacle.reshape(nz * nx, ny),
    )
    return out[0].reshape(3, nz, nx, ny), out[1].reshape(nz, nx, ny)


def solution(mesh):
    placed = (P(None, None, "gx", "gy"), P(None, None, "gx", "gy"), P(None, "gx", "gy"))
    return jax.shard_map(
        functools.partial(body, mesh.shape["gx"], mesh.shape["gy"]),
        mesh=mesh,
        in_specs=placed,
        out_specs=(P(None, None, "gx", "gy"), P(None, "gx", "gy")),
        check_vma=False,
    )
```

```python
import functools

import jax
import jax.numpy as jnp
from jax import lax
from jax.experimental import pallas as pl
from jax.experimental.pallas import tpu as pltpu
from jax.sharding import PartitionSpec as P

LEVELS = 3
SWEEPS = 2
COARSE_SWEEPS = 8
VISCOSITY = 0.1
TIME_STEP = 0.25
WEIGHT_NEW = 15.0 / 16.0
WEIGHT_OLD = -25.0 / 48.0
HELMHOLTZ = 0.0001

LANES = 128
SUB = 8
HALO_X = 8
HALO_Y = 24
MESH = pl.DeviceIdType.MESH


def iota2(shape, dim):
    return lax.broadcasted_iota(jnp.int32, shape, dim)


def restrict_matrix(rows, cols, nz, period):
    i, o = iota2((rows, cols), 0), iota2((rows, cols), 1)
    o = o % period
    half = nz // 2
    hit = ((i // nz) // 2 == o // half) & ((i % nz) // 2 == o % half)
    return jnp.where(hit, 0.125, 0.0).astype(jnp.float32)


def prolong_matrix(rows, cols, nz):
    i, o = iota2((rows, cols), 0), iota2((rows, cols), 1)
    half = nz // 2
    hit = ((o // nz) // 2 == i // half) & ((o % nz) // 2 == i % half)
    return jnp.where(hit, 1.0, 0.0).astype(jnp.float32)


def mm(a, b):
    return jnp.dot(a, b, precision=lax.Precision.HIGHEST, preferred_element_type=jnp.float32)


class Level:
    def __init__(self, level, nz):
        self.nz = nz
        self.scale = 1.0 / float(4**level)
        lane = iota2((SUB, LANES), 1)
        row = iota2((SUB, LANES), 0)
        self.lane = lane
        self.row = row
        z = lane % nz
        self.not_top = z < nz - 1
        self.not_bottom = z > 0
        parity = (z + lane // nz + row) % 2
        self.colour = [parity == 0, parity == 1]
        edge = (z == 0) | (z == nz - 1)
        diag_in = HELMHOLTZ + 6.0 * self.scale
        diag_edge = HELMHOLTZ + 5.0 * self.scale
        self.diag = jnp.where(edge, diag_edge, diag_in).astype(jnp.float32)
        self.inv = jnp.where(edge, 1.0 / diag_edge, 1.0 / diag_in).astype(jnp.float32)
        self.take = jnp.where(
            edge, self.scale / diag_edge, self.scale / diag_in
        ).astype(jnp.float32)

    def x_plus(self, tiles, t):
        n = len(tiles)
        both = tiles[t] if n == 1 else jnp.where(self.lane < self.nz, tiles[(t + 1) % n], tiles[t])
        return pltpu.roll(both, LANES - self.nz, 1)

    def x_minus(self, tiles, t):
        n = len(tiles)
        last = self.lane >= LANES - self.nz
        both = tiles[t] if n == 1 else jnp.where(last, tiles[(t - 1) % n], tiles[t])
        return pltpu.roll(both, self.nz, 1)

    def y_plus(self, tile, following):
        return pltpu.roll(jnp.where(self.row == 0, following, tile), SUB - 1, 0)

    def y_minus(self, tile, previous):
        return pltpu.roll(jnp.where(self.row == SUB - 1, previous, tile), 1, 0)

    def z_plus(self, tile):
        return jnp.where(self.not_top, pltpu.roll(tile, LANES - 1, 1), 0.0)

    def z_minus(self, tile):
        return jnp.where(self.not_bottom, pltpu.roll(tile, 1, 1), 0.0)


def tile_of(t):
    return slice(t * LANES, (t + 1) * LANES)


def row_loop(tiles, unroll, body):
    while tiles % unroll:
        unroll -= 1

    def step(i, carry):
        for k in range(unroll):
            body(pl.multiple_of((i * unroll + k) * SUB, SUB))
        return carry

    lax.fori_loop(0, tiles // unroll, step, 0)


def neighbours(lv, p, r, tiles, t):
    cols = tile_of(t)
    here = tiles[t]
    up = lv.y_plus(here, p[pl.ds(r + 2 * SUB, SUB), cols])
    down = lv.y_minus(here, p[pl.ds(r, SUB), cols])
    return (
        lv.x_plus(tiles, t)
        + lv.x_minus(tiles, t)
        + up
        + down
        + lv.z_plus(here)
        + lv.z_minus(here)
    )


def wrap_rows(p):
    rows = p.shape[0]
    p[0:SUB, :] = p[rows - 2 * SUB : rows - SUB, :]
    p[rows - SUB : rows, :] = p[SUB : 2 * SUB, :]


def first_half(lv, p, f, unroll):
    def body(r):
        for t in range(p.shape[1] // LANES):
            p[pl.ds(r + SUB, SUB), tile_of(t)] = jnp.where(
                lv.colour[0], f[pl.ds(r, SUB), tile_of(t)] * lv.inv, 0.0
            )

    row_loop(f.shape[0] // SUB, unroll, body)


def half_sweep(lv, p, f, colour, unroll, wrap, trim_rows=0, trim_tiles=0):
    if wrap:
        wrap_rows(p)
    count = p.shape[1] // LANES

    def body(start):
        r = start + trim_rows
        tiles = [p[pl.ds(r + SUB, SUB), tile_of(t)] for t in range(count)]
        for t in range(trim_tiles, count - trim_tiles):
            total = neighbours(lv, p, r, tiles, t)
            new = f[pl.ds(r, SUB), tile_of(t)] * lv.inv + total * lv.take
            p[pl.ds(r + SUB, SUB), tile_of(t)] = (
                jnp.where(lv.colour[0], tiles[t], new) if colour else jnp.where(lv.colour[0], new, tiles[t])
            )

    row_loop((f.shape[0] - 2 * trim_rows) // SUB, unroll, body)


def presmooth(lv, p, f, sweeps, unroll, wrap):
    first_half(lv, p, f, unroll)
    for k in range(1, 2 * sweeps):
        half_sweep(lv, p, f, k % 2, unroll, wrap)


def postsmooth(lv, p, f, unroll, wrap, trim_rows=0, trim_tiles=0):
    for k in range(2 * SWEEPS):
        half_sweep(lv, p, f, k % 2, unroll, wrap, trim_rows, trim_tiles)


def residual(lv, p, f, out, first, last, unroll, wrap):
    if wrap:
        wrap_rows(p)
    count = p.shape[1] // LANES

    def body(r):
        tiles = [p[pl.ds(r + SUB, SUB), tile_of(t)] for t in range(count)]
        for t in range(first, last):
            total = neighbours(lv, p, r, tiles, t)
            out[pl.ds(r, SUB), tile_of(t - first)] = f[pl.ds(r, SUB), tile_of(t)] - (
                lv.diag * tiles[t] - lv.scale * total
            )

    row_loop(f.shape[0] // SUB, unroll, body)


def restrict_rows(value, pairs, start, count, emit):
    for t in range(value.shape[1] // LANES):
        pairs[t, 0 : value.shape[0], :] = value[:, tile_of(t)]
        emit(
            t,
            pairs[t, pl.ds(start, count, stride=2), :]
            + pairs[t, pl.ds(start + 1, count, stride=2), :],
        )


def prolong_rows(value, pairs, p, first):
    rows = value.shape[0]
    for k in range(value.shape[1] // LANES):
        t = first + k
        pairs[t, pl.ds(0, rows, stride=2), :] = value[:, tile_of(k)]
        pairs[t, pl.ds(1, rows, stride=2), :] = value[:, tile_of(k)]
        p[SUB : SUB + 2 * rows, tile_of(t)] += pairs[t, 0 : 2 * rows, :]


def kernel(
    nx_dev, ny_dev, nz, nx, ny,
    vel_in, old_in, obs_in, cor_out, pre_out,
    vel, old, fluid, edge, edge_in, pred,
    f0, p0, r0, f1, p1, r1, f2, p2, r2, f3, p3, pairs,
    send_sem, recv_sem,
):
    gx, gy = lax.axis_index("gx"), lax.axis_index("gy")

    def device(dx, dy):
        return (lax.rem(gx + dx + nx_dev, nx_dev), lax.rem(gy + dy + ny_dev, ny_dev))

    peers = [(d, 0) for d in range(1, nx_dev)] + [(0, d) for d in range(1, ny_dev)]
    peers += [(a, b) for a in (-1, 1) for b in (-1, 1)]
    barrier = pltpu.get_barrier_semaphore()
    for dx, dy in peers:
        pl.semaphore_signal(barrier, inc=1, device_id=device(dx, dy), device_id_type=MESH)

    number = [0]

    def send(src, dst, dx, dy):
        k = number[0]
        number[0] += 1
        copy = pltpu.make_async_remote_copy(
            src_ref=src, dst_ref=dst, send_sem=send_sem.at[k], recv_sem=recv_sem.at[k],
            device_id=device(dx, dy), device_id_type=MESH,
        )
        copy.start()
        return copy

    per = LANES // nz
    blocks = nx // per
    width = blocks * LANES
    lv0 = Level(0, nz)
    lane = lv0.lane

    def load_tile(ref, base, t):
        rows = [ref[pl.ds(base + t * per + i, nz, stride=nx), :] for i in range(per)]
        return jnp.concatenate(rows, axis=0).T

    for c in range(3):
        for t in range(blocks):
            vel[c, SUB : SUB + ny, tile_of(t + 1)] = load_tile(vel_in, c * nz * nx, t)

    pltpu_wait = functools.partial(pl.semaphore_wait, barrier)
    pltpu_wait(len(peers))

    def join(high):
        parts = []
        for c in range(3):
            source = vel[c, SUB : SUB + ny, tile_of(blocks if high else 1)]
            start = LANES - nz if high else 0
            parts.append(pltpu.roll(source, (c * nz - start) % LANES, 1))
        wide = iota2((ny, LANES), 1)
        return jnp.where(wide < nz, parts[0], jnp.where(wide < 2 * nz, parts[1], parts[2]))

    copies = [
        send(vel.at[:, ny : ny + SUB, LANES : LANES + width], vel.at[:, 0:SUB, LANES : LANES + width], 0, 1),
        send(
            vel.at[:, SUB : 2 * SUB, LANES : LANES + width],
            vel.at[:, SUB + ny : 2 * SUB + ny, LANES : LANES + width], 0, -1,
        ),
    ]
    edge[0] = join(True)
    copies.append(send(edge.at[0], edge_in.at[0], 1, 0))
    edge[1] = join(False)
    copies.append(send(edge.at[1], edge_in.at[1], -1, 0))

    for c in range(3):
        for t in range(blocks):
            old[c, :, tile_of(t)] = load_tile(old_in, c * nz * nx, t)
    for t in range(blocks):
        fluid[:, tile_of(t)] = (1 - load_tile(obs_in, 0, t)).astype(jnp.float32)
    for copy in copies:
        copy.wait()
    for c in range(3):
        vel[c, SUB : SUB + ny, tile_of(0)] = pltpu.roll(edge_in[0], (LANES - nz - c * nz) % LANES, 1)
        vel[c, SUB : SUB + ny, tile_of(blocks + 1)] = pltpu.roll(edge_in[1], (-c * nz) % LANES, 1)

    def momentum(r):
        here = [
            [vel[c, pl.ds(r + SUB, SUB), tile_of(t)] for t in range(blocks + 2)] for c in range(3)
        ]
        for t in range(1, blocks + 1):
            cols = tile_of(t)
            wet = fluid[pl.ds(r, SUB), tile_of(t - 1)]
            for c in range(3):
                q = here[c][t]
                xp, xm = lv0.x_plus(here[c], t), lv0.x_minus(here[c], t)
                yp = lv0.y_plus(q, vel[c, pl.ds(r + 2 * SUB, SUB), cols])
                ym = lv0.y_minus(q, vel[c, pl.ds(r, SUB), cols])
                zp, zm = lv0.z_plus(q), lv0.z_minus(q)
                advect = 0.5 * (
                    here[0][t] * (xp - xm) + here[1][t] * (yp - ym) + here[2][t] * (zp - zm)
                )
                diffuse = xp + xm + yp + ym + zp + zm - 6.0 * q
                tendency = VISCOSITY * diffuse - advect
                pred[c, pl.ds(r + SUB, SUB), cols] = wet * (
                    q
                    + TIME_STEP
                    * (WEIGHT_NEW * tendency + WEIGHT_OLD * old[c, pl.ds(r, SUB), tile_of(t - 1)])
                )

    row_loop(ny // SUB, 2, momentum)

    inner = slice(LANES, LANES + width)
    copies = [
        send(pred.at[0, SUB : SUB + ny, tile_of(blocks)], pred.at[0, SUB : SUB + ny, tile_of(0)], 1, 0),
        send(pred.at[0, SUB : SUB + ny, tile_of(1)], pred.at[0, SUB : SUB + ny, tile_of(blocks + 1)], -1, 0),
        send(pred.at[1, ny : ny + SUB, inner], pred.at[1, 0:SUB, inner], 0, 1),
        send(pred.at[1, SUB : 2 * SUB, inner], pred.at[1, SUB + ny : 2 * SUB + ny, inner], 0, -1),
    ]
    for copy in copies:
        copy.wait()

    side = HALO_X // per
    hx = side * LANES

    def divergence(r):
        u = [pred[0, pl.ds(r + SUB, SUB), tile_of(t)] for t in range(blocks + 2)]
        for t in range(1, blocks + 1):
            cols = tile_of(t)
            v = pred[1, pl.ds(r + SUB, SUB), cols]
            w = pred[2, pl.ds(r + SUB, SUB), cols]
            v_plus = lv0.y_plus(v, pred[1, pl.ds(r + 2 * SUB, SUB), cols])
            v_minus = lv0.y_minus(v, pred[1, pl.ds(r, SUB), cols])
            total = (
                (lv0.x_plus(u, t) - lv0.x_minus(u, t))
                + (v_plus - v_minus)
                + (lv0.z_plus(w) - lv0.z_minus(w))
            )
            f0[pl.ds(r + HALO_Y, SUB), tile_of(t - 1 + side)] = total * (-0.5 / TIME_STEP)

    row_loop(ny // SUB, 2, divergence)

    span = {
        0: (slice(HALO_Y, HALO_Y + ny), slice(HALO_Y, HALO_Y + ny)),
        1: (slice(ny, ny + HALO_Y), slice(0, HALO_Y)),
        -1: (slice(HALO_Y, 2 * HALO_Y), slice(HALO_Y + ny, 2 * HALO_Y + ny)),
    }
    cross = {
        0: (slice(hx, hx + width), slice(hx, hx + width)),
        1: (slice(width, width + hx), slice(0, hx)),
        -1: (slice(hx, 2 * hx), slice(hx + width, 2 * hx + width)),
    }
    copies = []
    for dx, dy in ((1, 0), (-1, 0), (0, 1), (0, -1), (1, 1), (1, -1), (-1, 1), (-1, -1)):
        copies.append(
            send(f0.at[span[dy][0], cross[dx][0]], f0.at[span[dy][1], cross[dx][1]], dx, dy)
        )
    lv1, lv2, lv3 = Level(1, nz // 2), Level(2, nz // 4), Level(3, nz // 8)
    zero_rows = jnp.zeros((SUB, p0.shape[1]), jnp.float32)
    p0[0:SUB, :] = zero_rows
    p0[p0.shape[0] - SUB :, :] = zero_rows
    p1[0:SUB, :] = zero_rows[:, : p1.shape[1]]
    p1[p1.shape[0] - SUB :, :] = zero_rows[:, : p1.shape[1]]
    for copy in copies:
        copy.wait()

    presmooth(lv0, p0, f0, SWEEPS, 2, False)
    residual(lv0, p0, f0, r0, side, side + blocks, 2, False)
    rows1 = f1.shape[0]
    down1 = mm(r0[...], restrict_matrix(width, LANES, nz, LANES))

    def emit1(t, value):
        f1[:, tile_of(t)] = value

    restrict_rows(down1, pairs, 0, rows1, emit1)

    copies = [
        send(f1.at[:, tile_of(0)], f1.at[:, tile_of(j)], nx_dev - j, 0) for j in range(1, nx_dev)
    ]
    for copy in copies:
        copy.wait()
    presmooth(lv1, p1, f1, SWEEPS, 11, False)
    residual(lv1, p1, f1, r1, 0, nx_dev, 1, False)
    cols2 = f2.shape[1]
    down2 = mm(r1[...], restrict_matrix(r1.shape[1], cols2, nz // 2, cols2))
    own2 = ny // 4

    def emit2(t, value):
        f2[0:own2, tile_of(t)] = value

    restrict_rows(down2, pairs, HALO_Y // 2, own2, emit2)
    copies = [
        send(f2.at[0:own2, :], f2.at[j * own2 : (j + 1) * own2, :], 0, ny_dev - j)
        for j in range(1, ny_dev)
    ]
    for copy in copies:
        copy.wait()

    presmooth(lv2, p2, f2, SWEEPS, 16, True)
    residual(lv2, p2, f2, r2, 0, cols2 // LANES, 16, True)
    down3 = mm(r2[...], restrict_matrix(cols2, f3.shape[1], nz // 4, cols2 // 4))

    def emit3(t, value):
        f3[:, tile_of(t)] = value

    restrict_rows(down3, pairs, 0, f3.shape[0], emit3)
    presmooth(lv3, p3, f3, COARSE_SWEEPS, 16, True)
    rows3 = f3.shape[0]
    prolong_rows(
        mm(p3[SUB : SUB + rows3, :], prolong_matrix(p3.shape[1], cols2, nz // 4)), pairs, p2, 0
    )
    postsmooth(lv2, p2, f2, 16, True)
    wrap_rows(p2)

    first2 = SUB - HALO_Y // 4
    window = p2[first2 : first2 + rows1 // 2, :]
    prolong_rows(mm(window, prolong_matrix(cols2, r1.shape[1], nz // 2)), pairs, p1, 0)
    postsmooth(lv1, p1, f1, 11, False)

    lift = prolong_matrix(LANES, width, nz)
    body_rows = slice(SUB, SUB + rows1)
    prolong_rows(mm(p1[body_rows, tile_of(nx_dev - 1)], lift[:, width - hx :]), pairs, p0, 0)
    prolong_rows(mm(p1[body_rows, tile_of(0)], lift), pairs, p0, side)
    prolong_rows(mm(p1[body_rows, tile_of(1)], lift[:, :hx]), pairs, p0, side + blocks)
    postsmooth(lv0, p0, f0, 3, False, HALO_Y - SUB, side - 1)

    low = SUB + HALO_Y

    def correct(r):
        here = [
            p0[pl.ds(r + low, SUB), tile_of(t)] for t in range(side - 1, side + blocks + 1)
        ]
        for t in range(1, blocks + 1):
            cols = tile_of(t + side - 1)
            slope = (
                lv0.x_plus(here, t) - lv0.x_minus(here, t),
                lv0.y_plus(here[t], p0[pl.ds(r + low + SUB, SUB), cols])
                - lv0.y_minus(here[t], p0[pl.ds(r + low - SUB, SUB), cols]),
                lv0.z_plus(here[t]) - lv0.z_minus(here[t]),
            )
            wet = fluid[pl.ds(r, SUB), tile_of(t - 1)]
            for c in range(3):
                old[c, pl.ds(r, SUB), tile_of(t - 1)] = wet * (
                    pred[c, pl.ds(r + SUB, SUB), tile_of(t)] - (0.5 * TIME_STEP) * slope[c]
                )

    row_loop(ny // SUB, 2, correct)

    def store_tile(ref, base, t, value):
        turned = value.T
        for i in range(per):
            ref[pl.ds(base + t * per + i, nz, stride=nx), :] = turned[i * nz : (i + 1) * nz, :]

    for t in range(blocks):
        store_tile(pre_out, 0, t, p0[low : low + ny, tile_of(t + side)])
    for c in range(3):
        for t in range(blocks):
            store_tile(cor_out, c * nz * nx, t, old[c, :, tile_of(t)])


def body(nx_dev, ny_dev, velocity, old_tendency, obstacle):
    _, nz, nx, ny = velocity.shape
    rows0 = ny + 2 * HALO_Y
    wide0 = (nx + 2 * HALO_X) * nz
    width = nx * nz
    rows1, wide1 = rows0 // 2, nx_dev * (nx // 2) * (nz // 2)
    rows2, wide2 = ny_dev * ny // 4, nx_dev * (nx // 4) * (nz // 4)
    rows3 = rows2 // 2
    wide3 = max(LANES, wide2 // 4)
    tall = max(rows0, rows1, rows2)
    count = max(wide0, wide1, wide2, wide3) // LANES
    copies = 4 + 4 + 8 + (nx_dev - 1) + (ny_dev - 1)
    f32 = jnp.float32
    out = pl.pallas_call(
        functools.partial(kernel, nx_dev, ny_dev, nz, nx, ny),
        out_shape=(
            jax.ShapeDtypeStruct((3 * nz * nx, ny), f32),
            jax.ShapeDtypeStruct((nz * nx, ny), f32),
        ),
        in_specs=[pl.BlockSpec(memory_space=pltpu.VMEM)] * 3,
        out_specs=[pl.BlockSpec(memory_space=pltpu.VMEM)] * 2,
        scratch_shapes=[
            pltpu.VMEM((3, ny + 2 * SUB, width + 2 * LANES), f32),
            pltpu.VMEM((3, ny, width), f32),
            pltpu.VMEM((ny, width), f32),
            pltpu.VMEM((2, ny, LANES), f32),
            pltpu.VMEM((2, ny, LANES), f32),
            pltpu.VMEM((3, ny + 2 * SUB, width + 2 * LANES), f32),
            pltpu.VMEM((rows0, wide0), f32),
            pltpu.VMEM((rows0 + 2 * SUB, wide0), f32),
            pltpu.VMEM((rows0, width), f32),
            pltpu.VMEM((rows1, wide1), f32),
            pltpu.VMEM((rows1 + 2 * SUB, wide1), f32),
            pltpu.VMEM((rows1, wide1), f32),
            pltpu.VMEM((rows2, wide2), f32),
            pltpu.VMEM((rows2 + 2 * SUB, wide2), f32),
            pltpu.VMEM((rows2, wide2), f32),
            pltpu.VMEM((rows3, wide3), f32),
            pltpu.VMEM((rows3 + 2 * SUB, wide3), f32),
            pltpu.VMEM((count, tall, LANES), f32),
            pltpu.SemaphoreType.DMA((copies,)),
            pltpu.SemaphoreType.DMA((copies,)),
        ],
        compiler_params=pltpu.CompilerParams(
            collective_id=0, has_side_effects=True, vmem_limit_bytes=60 * 1024 * 1024
        ),
    )(
        velocity.reshape(3 * nz * nx, ny),
        old_tendency.reshape(3 * nz * nx, ny),
        obstacle.reshape(nz * nx, ny),
    )
    return out[0].reshape(3, nz, nx, ny), out[1].reshape(nz, nx, ny)


def solution(mesh):
    placed = (P(None, None, "gx", "gy"), P(None, None, "gx", "gy"), P(None, "gx", "gy"))
    return jax.shard_map(
        functools.partial(body, mesh.shape["gx"], mesh.shape["gy"]),
        mesh=mesh,
        in_specs=placed,
        out_specs=(P(None, None, "gx", "gy"), P(None, "gx", "gy")),
        check_vma=False,
    )
```
